256 devices in a mesh: rec: 32 (over z, x), ani: 4 (over y_lo, core), chain: 2 (over y_hi).
Axes of the slice: x: 4, y: 4 (y_hi: 2, y_lo: 2; y = y_hi * 2 + y_lo), z: 8, core: 2. Of those that a mesh axis runs over, the one named last changes fastest.
Arguments:
- genotypes: bfloat16 [131072, 4096], P('ani', 'rec'), may hold values from -0.09375 to 0.09375
- effects: float32 [8192], P(('chain', 'rec')), parts along dimension 0, may hold values from -6 to 6
- gaussian_draw: float32 [8192], P(('chain', 'rec')), parts along dimension 0, may hold values from -6 to 6
- prior_prec: float32 [4096], P('rec'), may hold values from 2 to 40
- accept: int32 [64], P(('chain', 'rec')), parts along dimension 0, may hold values 0 or 1
- herd_effect: float32 [131072], P(('chain', 'rec')), parts along dimension 0, may hold values from -6 to 6
- phenotype: float32 [1048576], P(('rec', 'ani')), may hold values from -12 to 12
- record_animal: int32 [1048576], P(('rec', 'ani')), may hold values from 0 to 131071
- record_bin: int32 [1048576], P(('rec', 'ani')), may hold values from 0 to 65535, as said below
- live_records: int32 [128], P(('rec', 'ani')), may hold values from 1 to 8192, 655360 in all
Outputs:
- next_effects: float32 [8192], P(('chain', 'rec')), parts along dimension 0
- resid_sum: float32 [262144], P(('chain', 'ani')), parts along dimension 0
The draws below stay inside these ranges and needn't reach their ends.
There are 2 independent parts, one for each index of `chain`. The reference program is written for one: setup_inputs(seed, part) draws one part's arguments, and reference() takes and returns one part's arrays. A program takes and returns all parts, laid end to end along the dimension named above; an argument that names none is the same for every part. Nothing has to cross between parts.
Inputs may be any that keep to these rules, and one draw needn't show every extreme that they name: `record_bin`: a record held by rec index k names a group of k * 2048 to (k + 1) * 2048 - 1.
All inputs are finite; a program needn't handle non-finite values. No bound on the sum of `accept` or of `live_records` on one device may be relied on, other than what follows from the above.
Results may differ from the reference program's by a relative error of at most 0.0033.
Values sent between devices are 32-bit elements; how exact they have to be, the bound alone decides.
A program may use at most 64 MiB of HBM per device.

```python
import math
import jax
import jax.numpy as jnp
import numpy as np

M = 4096
BLOCK = 128
RD = 8192
HB = 2048
ANIMALS = 131072
SHARD_RECS = 32768
RECORDS = 1048576
BINS = 65536
N_REC = 32
N_ANI = 4


def draw_record_bin(key, part):
    position = jnp.arange(RECORDS, dtype=jnp.int32)
    shard = position // SHARD_RECS
    offset = jax.random.randint(key, (RECORDS,), 0, HB, dtype=jnp.int32)
    return shard * HB + offset


def touch_ends(array, stream_key, smallest, high):
    longest = array.shape.index(max(array.shape))
    spots = []
    for shift in (0, 1):
        where = [jax.random.randint(jax.random.fold_in(stream_key, axis), (), 0, length) for axis, length in enumerate(array.shape)]
        where[longest] = (where[longest] + shift) % array.shape[longest]
        spots.append(tuple(where))
    return array.at[spots[0]].set(smallest).at[spots[1]].set(high)


def levels(rng, extent, cuts, least, largest):
    loudness = 1.0
    for dim, blocks in cuts:
        heights = jax.random.uniform(jax.random.fold_in(jax.random.fold_in(rng, 6), dim), (blocks,), jnp.float32, least / len(cuts), largest / len(cuts))
        loudness = loudness * jnp.repeat(jnp.exp(heights), extent[dim] // blocks).reshape((-1,) + (1,) * (len(extent) - 1 - dim))
    return loudness


def length_profile(number_of, total, bound, slope):
    portions = [(1 << 20) // math.isqrt(standing ** slope) + 1 for standing in range(2, number_of + 1)]
    spare, given = total - bound - (number_of - 1), [1] * (number_of - 1)
    while spare > 0:
        free = [i for i in range(number_of - 1) if given[i] < bound]
        whole, left = sum([portions[i] for i in free]), spare
        for i in free:
            more = min(bound - given[i], max(1, left * portions[i] // whole), spare)
            given[i] = given[i] + more
            spare = spare - more
    return np.array([bound] + given)


def ragged(stream_key, amount, total, reach, skew):
    if amount == 2:
        one = jax.random.randint(stream_key, (), max(1, total - reach), min(reach, total - 1) + 1)
        return jnp.stack([one, total - one])
    tallies = jnp.asarray(length_profile(amount, total, reach, skew), jnp.int32)
    pairs = (amount - 1) // 2
    source_of, sink = tallies[1:1 + 2 * pairs:2], tallies[2:2 + 2 * pairs:2]
    margin = jnp.minimum(source_of - 1, reach - sink)
    passed = jax.random.randint(jax.random.fold_in(stream_key, 1), (pairs,), 0, 1 << 20) % (margin + 1)
    tallies = tallies.at[1:1 + 2 * pairs:2].set(source_of - passed).at[2:2 + 2 * pairs:2].set(sink + passed)
    return tallies[jax.random.permutation(jax.random.fold_in(stream_key, 2), amount)]


def noise(key, dims, spread, limit, cuts=(), kind=jnp.bfloat16):
    result = jax.random.normal(key, dims, jnp.float32) * spread
    if len(cuts) > 0:
        result = levels(key, dims, cuts, -0.22, 0.18) * result
    return jnp.clip(result, min=-limit, max=limit).astype(kind)


def setup_inputs(seed: int = 0, part: int = 0) -> dict:
    key_list = jax.random.split(jax.random.key(seed), 11)
    part_keys = jax.random.split(jax.random.fold_in(key_list[10], part), 11)
    return {
        "genotypes": noise(key_list[0], (ANIMALS, M), M ** -0.5, 0.09375, ((0, 4), (1, 32))),
        "effects": noise(part_keys[1], (M,), 1.0, 6.0, ((0, 32),), jnp.float32),
        "gaussian_draw": noise(part_keys[2], (M,), 1.0, 6.0, ((0, 32),), jnp.float32),
        "prior_prec": jnp.clip(jnp.exp(math.log(40.0) - 2.9957323 * jax.random.uniform(key_list[3], (M,), jnp.float32) ** levels(key_list[3], (M,), ((0, 32),), -0.2, 0.2)), 2.0, 40.0),
        "accept": touch_ends((jax.random.randint(part_keys[4], (M // BLOCK,), 0, 4) < 3).astype(jnp.int32), jax.random.fold_in(part_keys[4], 1), 0, 1),
        "herd_effect": noise(part_keys[5], (BINS,), 1.0, 6.0, ((0, 32),), jnp.float32),
        "phenotype": noise(key_list[6], (RECORDS,), 2.0, 12.0, ((0, 128),), jnp.float32),
        "record_animal": touch_ends(jax.random.randint(key_list[7], (RECORDS,), 0, ANIMALS), jax.random.fold_in(key_list[7], 1), 0, ANIMALS - 1).astype(jnp.int32),
        "record_bin": draw_record_bin(jax.random.fold_in(key_list[10], 71), part),
        "live_records": ragged(key_list[9], N_REC * N_ANI, RD * N_REC * N_ANI * 5 // 8, RD, 2).astype(jnp.int32),
    }


def reference(genotypes, effects, gaussian_draw, prior_prec, accept, herd_effect, phenotype, record_animal, record_bin, live_records):
    step_size = 0.005
    effects_half = effects.astype(jnp.bfloat16)
    breeding = jnp.dot(genotypes, effects_half, preferred_element_type=jnp.float32)
    position = jnp.arange(RECORDS, dtype=jnp.int32)
    live = position % RD < jnp.take(live_records, position // RD)
    residual = jnp.where(live, phenotype - jnp.take(herd_effect, record_bin) - jnp.take(breeding, record_animal), jnp.zeros_like(phenotype))
    resid_sum = jax.ops.segment_sum(residual, record_animal, num_segments=ANIMALS)
    resid_half = resid_sum.astype(jnp.bfloat16)
    gradient = jnp.dot(resid_half, genotypes, preferred_element_type=jnp.float32) - prior_prec * effects
    proposal = effects + step_size * gradient + math.sqrt(2.0 * step_size) * gaussian_draw
    accepted = jnp.repeat(accept, BLOCK) == 1
    return (jnp.where(accepted, proposal, effects), resid_sum)
```

```python
import math

import jax
import jax.numpy as jnp
from jax import lax
from jax.experimental import pallas as pl
from jax.experimental.pallas import tpu as pltpu
from jax.sharding import PartitionSpec as P

BLOCK = 128
W = 1024
NX, NZ = 4, 8
F32, BF16 = jnp.float32, jnp.bfloat16


def row_kernel(first_ref, live_ref, phen_ref, animal_ref, bin_ref, herd_ref, out_ref):
    t = herd_ref[...]
    t1 = t.astype(BF16)
    r = t - t1.astype(F32)
    t2 = r.astype(BF16)
    t3 = (r - t2.astype(F32)).astype(BF16)
    table = jnp.concatenate([t1, t2, t3], axis=0)
    lo_iota = lax.broadcasted_iota(jnp.int32, (128, W), 0)
    hi_iota = lax.broadcasted_iota(jnp.int32, (16, W), 0)
    lane = lax.broadcasted_iota(jnp.int32, (1, W), 1)
    for i in range(phen_ref.shape[0]):
        b = bin_ref[i : i + 1, :] - first_ref[0]
        hi, lo = b >> 7, b & 127
        pick = jnp.where(lo_iota == lo, 1.0, 0.0).astype(BF16)
        g = jnp.dot(table, pick, preferred_element_type=F32)
        g = g[0:16] + g[16:32] + g[32:48]
        herd = jnp.sum(jnp.where(hi_iota == hi, g, 0.0), axis=0, keepdims=True)
        alive = lane + i * W < live_ref[0]
        out_ref[0, i : i + 1, :] = jnp.where(alive, phen_ref[i : i + 1, :] - herd, 0.0)
        out_ref[1, i : i + 1, :] = jnp.where(alive, animal_ref[i : i + 1, :], -1).astype(F32)


def scatter_kernel(first_ref, rec_ref, s_ref, n_ref, acc_ref):
    lo_iota = lax.broadcasted_iota(jnp.int32, (128, W), 0)
    hi_iota = lax.broadcasted_iota(jnp.int32, (256, W), 0)
    acc_ref[...] = jnp.zeros_like(acc_ref)

    def group(g, carry):
        for j in range(8):
            y = rec_ref[g, 0, j : j + 1, :]
            a = rec_ref[g, 1, j : j + 1, :].astype(jnp.int32) - first_ref[0]
            hi, lo = a >> 7, a & 127
            y1 = y.astype(BF16)
            y2 = y - y1.astype(F32)
            y1 = y1.astype(F32)
            rows = jnp.where(hi_iota == hi, 1.0, 0.0).astype(BF16)
            hit = lo_iota == lo
            cols = jnp.concatenate(
                [
                    jnp.where(hit, y1, 0.0).astype(BF16),
                    jnp.where(hit, y2, 0.0).astype(BF16),
                    jnp.where(hit, 1.0, 0.0).astype(BF16),
                ],
                axis=0,
            )
            acc_ref[...] += lax.dot_general(
                cols, rows, (((1,), (1,)), ((), ())), preferred_element_type=F32
            )
        return carry

    lax.fori_loop(0, rec_ref.shape[0], group, 0)
    s_ref[...] = (acc_ref[0:128] + acc_ref[128:256]).T
    n_ref[...] = acc_ref[256:384].T


def exchange_kernel(b_ref, s_ref, n_ref, out_ref, r1, part, r2, s1, v1, s2, v2, s3, v3, s4, v4):
    me = lax.axis_index("rec")
    mz, mx = me // NX, me % NX

    def at_x(d):
        return (mx + d) % NX

    def at_z(d):
        return (mz + d) % NZ

    barrier = pltpu.get_barrier_semaphore()
    for d in range(1, NX):
        pl.semaphore_signal(barrier, inc=1, device_id={"rec": mz * NX + at_x(d)})
    for d in range(1, NZ):
        pl.semaphore_signal(barrier, inc=1, device_id={"rec": at_z(d) * NX + mx})
    pl.semaphore_wait(barrier, NX - 1 + NZ - 1)

    ins = (b_ref, s_ref, n_ref)
    copies = []
    for d in (2, 1, 3):
        for k in range(3):
            copies.append(
                pltpu.make_async_remote_copy(
                    ins[k].at[at_x(d)], r1.at[d - 1, k], s1.at[d - 1, k], v1.at[d - 1, k],
                    device_id={"rec": mz * NX + at_x(d)},
                )
            )
            copies[-1].start()
    for c in copies:
        c.wait_recv()
    for k in range(3):
        part[:, k] = (ins[k][mx] + r1[0, k]) + (r1[1, k] + r1[2, k])
    for c in copies:
        c.wait_send()

    copies = []
    for d in (4, 3, 5, 2, 6, 1, 7):
        copies.append(
            pltpu.make_async_remote_copy(
                part.at[at_z(d)], r2.at[d - 1], s2.at[d - 1], v2.at[d - 1],
                device_id={"rec": at_z(d) * NX + mx},
            )
        )
        copies[-1].start()
    for c in copies:
        c.wait_recv()
    total = part[mz]
    for d in range(NZ - 1):
        total = total + r2[d]
    out_ref[mx, mz] = total[1] - total[2] * total[0]
    for c in copies:
        c.wait_send()

    copies = []
    for d in (4, 3, 5, 2, 6, 1, 7):
        copies.append(
            pltpu.make_async_remote_copy(
                out_ref.at[mx, mz], out_ref.at[mx, mz], s3.at[d - 1], v3.at[d - 1],
                device_id={"rec": at_z(d) * NX + mx},
            )
        )
        copies[-1].start()
    for d in range(1, NZ):
        pltpu.make_async_remote_copy(
            out_ref.at[mx, at_z(NZ - d)], out_ref.at[mx, at_z(NZ - d)], s3.at[d - 1], v3.at[d - 1],
            device_id={"rec": at_z(d) * NX + mx},
        ).wait_recv()
    for c in copies:
        c.wait_send()

    copies = []
    for d in (2, 1, 3):
        copies.append(
            pltpu.make_async_remote_copy(
                out_ref.at[mx], out_ref.at[mx], s4.at[d - 1], v4.at[d - 1],
                device_id={"rec": mz * NX + at_x(d)},
            )
        )
        copies[-1].start()
    for d in range(1, NX):
        pltpu.make_async_remote_copy(
            out_ref.at[at_x(NX - d)], out_ref.at[at_x(NX - d)], s4.at[d - 1], v4.at[d - 1],
            device_id={"rec": mz * NX + at_x(d)},
        ).wait_recv()
    for c in copies:
        c.wait_send()


VM = pl.BlockSpec(memory_space=pltpu.VMEM)
SM = pl.BlockSpec(memory_space=pltpu.SMEM)


def shape(*dims):
    return jax.ShapeDtypeStruct(dims, F32)


def on_device(
    genotypes, effects, gaussian_draw, prior_prec, accept,
    herd_effect, phenotype, record_animal, record_bin, live_records,
):
    step_size = 0.005
    rd, own = phenotype.shape[0], genotypes.shape[0]
    first_bin = (lax.axis_index("rec") * herd_effect.shape[0]).astype(jnp.int32).reshape(1)
    first_animal = (lax.axis_index("ani") * own).astype(jnp.int32).reshape(1)
    rows = pl.pallas_call(
        row_kernel,
        out_shape=shape(2, rd // W, W),
        in_specs=[SM, SM, VM, VM, VM, VM],
        out_specs=VM,
    )(
        first_bin, live_records, phenotype.reshape(-1, W), record_animal.reshape(-1, W),
        record_bin.reshape(-1, W), herd_effect.reshape(16, 128),
    )
    records = lax.all_gather(rows, "ani", axis=0)
    breeding = jnp.dot(genotypes, effects.astype(BF16), preferred_element_type=F32)
    s, n = pl.pallas_call(
        scatter_kernel,
        out_shape=(shape(own // 128, 128), shape(own // 128, 128)),
        in_specs=[SM, VM],
        out_specs=(VM, VM),
        scratch_shapes=[pltpu.VMEM((384, 256), F32)],
    )(first_animal, records)
    dma = pltpu.SemaphoreType.DMA
    part = (NX, NZ, 8, 128)
    resid_sum = pl.pallas_call(
        exchange_kernel,
        out_shape=shape(*part),
        in_specs=[VM, VM, VM],
        out_specs=VM,
        scratch_shapes=[
            pltpu.VMEM((NX - 1, 3, NZ, 8, 128), F32),
            pltpu.VMEM((NZ, 3, 8, 128), F32),
            pltpu.VMEM((NZ - 1, 3, 8, 128), F32),
            dma((NX - 1, 3)), dma((NX - 1, 3)),
            dma((NZ - 1,)), dma((NZ - 1,)),
            dma((NZ - 1,)), dma((NZ - 1,)),
            dma((NX - 1,)), dma((NX - 1,)),
        ],
        compiler_params=pltpu.CompilerParams(collective_id=0, has_side_effects=True),
    )(breeding.reshape(part), s.reshape(part), n.reshape(part)).reshape(own)
    grad_part = jnp.dot(resid_sum.astype(BF16), genotypes, preferred_element_type=F32)
    gradient = lax.psum(grad_part, "ani") - prior_prec * effects
    proposal = effects + step_size * gradient + math.sqrt(2.0 * step_size) * gaussian_draw
    accepted = jnp.repeat(accept, BLOCK) == 1
    return (jnp.where(accepted, proposal, effects), resid_sum)


def solution(mesh):
    return jax.shard_map(
        on_device,
        mesh=mesh,
        in_specs=(
            P("ani", "rec"),
            P(("chain", "rec")),
            P(("chain", "rec")),
            P("rec"),
            P(("chain", "rec")),
            P(("chain", "rec")),
            P(("rec", "ani")),
            P(("rec", "ani")),
            P(("rec", "ani")),
            P(("rec", "ani")),
        ),
        out_specs=(P(("chain", "rec")), P(("chain", "ani"))),
        check_vma=False,
    )
```

```python
import math

import jax
import jax.numpy as jnp
from jax import lax
from jax.experimental import pallas as pl
from jax.experimental.pallas import tpu as pltpu
from jax.sharding import PartitionSpec as P

BLOCK = 128
W = 1024
NA = 4
NX, NZ = 4, 8
F32, BF16 = jnp.float32, jnp.bfloat16


def row_kernel(first_ref, live_ref, phen_ref, animal_ref, bin_ref, herd_ref, out_ref):
    t = herd_ref[...]
    t1 = t.astype(BF16)
    r = t - t1.astype(F32)
    t2 = r.astype(BF16)
    t3 = (r - t2.astype(F32)).astype(BF16)
    table = jnp.concatenate([t1, t2, t3], axis=0)
    lo_iota = lax.broadcasted_iota(jnp.int32, (128, W), 0)
    hi_iota = lax.broadcasted_iota(jnp.int32, (16, W), 0)
    lane = lax.broadcasted_iota(jnp.int32, (1, W), 1)
    for i in range(phen_ref.shape[0]):
        b = bin_ref[i : i + 1, :] - first_ref[0]
        hi, lo = b >> 7, b & 127
        pick = jnp.where(lo_iota == lo, 1.0, 0.0).astype(BF16)
        g = jnp.dot(table, pick, preferred_element_type=F32)
        g = g[0:16] + g[16:32] + g[32:48]
        herd = jnp.sum(jnp.where(hi_iota == hi, g, 0.0), axis=0, keepdims=True)
        alive = lane + i * W < live_ref[0]
        out_ref[0, i : i + 1, :] = jnp.where(alive, phen_ref[i : i + 1, :] - herd, 0.0)
        out_ref[1, i : i + 1, :] = jnp.where(alive, animal_ref[i : i + 1, :], -1).astype(F32)


def scatter_kernel(first_ref, rec_ref, s_ref, n_ref, acc_ref):
    lo_iota = lax.broadcasted_iota(jnp.int32, (128, W), 0)
    hi_iota = lax.broadcasted_iota(jnp.int32, (256, W), 0)
    acc_ref[...] = jnp.zeros_like(acc_ref)

    def group(g, carry):
        for j in range(8):
            y = rec_ref[g, 0, j : j + 1, :]
            a = rec_ref[g, 1, j : j + 1, :].astype(jnp.int32) - first_ref[0]
            hi, lo = a >> 7, a & 127
            y1 = y.astype(BF16)
            y2 = y - y1.astype(F32)
            y1 = y1.astype(F32)
            rows = jnp.where(hi_iota == hi, 1.0, 0.0).astype(BF16)
            hit = lo_iota == lo
            cols = jnp.concatenate(
                [
                    jnp.where(hit, y1, 0.0).astype(BF16),
                    jnp.where(hit, y2, 0.0).astype(BF16),
                    jnp.where(hit, 1.0, 0.0).astype(BF16),
                ],
                axis=0,
            )
            acc_ref[...] += lax.dot_general(
                cols, rows, (((1,), (1,)), ((), ())), preferred_element_type=F32
            )
        return carry

    lax.fori_loop(0, rec_ref.shape[0], group, 0)
    s_ref[...] = (acc_ref[0:128] + acc_ref[128:256]).T
    n_ref[...] = acc_ref[256:384].T


def exchange_kernel(b_ref, s_ref, n_ref, out_ref, r1, part, r2, s1, v1, s2, v2, s3, v3, s4, v4):
    me = lax.axis_index("rec")
    mz, mx = me // NX, me % NX

    def at_x(d):
        return (mx + d) % NX

    def at_z(d):
        return (mz + d) % NZ

    barrier = pltpu.get_barrier_semaphore()
    for d in range(1, NX):
        pl.semaphore_signal(barrier, inc=1, device_id={"rec": mz * NX + at_x(d)})
    for d in range(1, NZ):
        pl.semaphore_signal(barrier, inc=1, device_id={"rec": at_z(d) * NX + mx})
    pl.semaphore_wait(barrier, NX - 1 + NZ - 1)

    ins = (b_ref, s_ref, n_ref)
    copies = []
    for d in (2, 1, 3):
        for k in range(3):
            copies.append(
                pltpu.make_async_remote_copy(
                    ins[k].at[at_x(d)], r1.at[d - 1, k], s1.at[d - 1, k], v1.at[d - 1, k],
                    device_id={"rec": mz * NX + at_x(d)},
                )
            )
            copies[-1].start()
    for c in copies:
        c.wait_recv()
    for k in range(3):
        part[:, k] = (ins[k][mx] + r1[0, k]) + (r1[1, k] + r1[2, k])
    for c in copies:
        c.wait_send()

    copies = []
    for d in (4, 3, 5, 2, 6, 1, 7):
        copies.append(
            pltpu.make_async_remote_copy(
                part.at[at_z(d)], r2.at[d - 1], s2.at[d - 1], v2.at[d - 1],
                device_id={"rec": at_z(d) * NX + mx},
            )
        )
        copies[-1].start()
    for c in copies:
        c.wait_recv()
    total = part[mz]
    for d in range(NZ - 1):
        total = total + r2[d]
    out_ref[mx, mz] = total[1] - total[2] * total[0]
    for c in copies:
        c.wait_send()

    copies = []
    for d in (4, 3, 5, 2, 6, 1, 7):
        copies.append(
            pltpu.make_async_remote_copy(
                out_ref.at[mx, mz], out_ref.at[mx, mz], s3.at[d - 1], v3.at[d - 1],
                device_id={"rec": at_z(d) * NX + mx},
            )
        )
        copies[-1].start()
    for d in range(1, NZ):
        pltpu.make_async_remote_copy(
            out_ref.at[mx, at_z(NZ - d)], out_ref.at[mx, at_z(NZ - d)], s3.at[d - 1], v3.at[d - 1],
            device_id={"rec": at_z(d) * NX + mx},
        ).wait_recv()
    for c in copies:
        c.wait_send()

    copies = []
    for d in (2, 1, 3):
        copies.append(
            pltpu.make_async_remote_copy(
                out_ref.at[mx], out_ref.at[mx], s4.at[d - 1], v4.at[d - 1],
                device_id={"rec": mz * NX + at_x(d)},
            )
        )
        copies[-1].start()
    for d in range(1, NX):
        pltpu.make_async_remote_copy(
            out_ref.at[at_x(NX - d)], out_ref.at[at_x(NX - d)], s4.at[d - 1], v4.at[d - 1],
            device_id={"rec": mz * NX + at_x(d)},
        ).wait_recv()
    for c in copies:
        c.wait_send()


VM = pl.BlockSpec(memory_space=pltpu.VMEM)
SM = pl.BlockSpec(memory_space=pltpu.SMEM)


def shape(*dims):
    return jax.ShapeDtypeStruct(dims, F32)


def greet(me, n):
    barrier = pltpu.get_barrier_semaphore()
    for d in range(1, n):
        pl.semaphore_signal(barrier, inc=1, device_id={"ani": (me + d) % n})
    pl.semaphore_wait(barrier, n - 1)


def spread_kernel(in_ref, out_ref, send, recv):
    n = out_ref.shape[0]
    me = lax.axis_index("ani")
    greet(me, n)
    copies = []
    for d in range(1, n):
        copies.append(
            pltpu.make_async_remote_copy(
                in_ref, out_ref.at[me], send.at[d - 1], recv.at[d - 1],
                device_id={"ani": (me + d) % n},
            )
        )
        copies[-1].start()
    out_ref[me] = in_ref[...]
    for d in range(1, n):
        src = (me + n - d) % n
        pltpu.make_async_remote_copy(
            in_ref, out_ref.at[src], send.at[d - 1], recv.at[d - 1],
            device_id={"ani": (me + d) % n},
        ).wait_recv()
    for c in copies:
        c.wait_send()


def spread(x, collective_id):
    n = NA
    return pl.pallas_call(
        spread_kernel,
        out_shape=shape(n, *x.shape),
        in_specs=[VM],
        out_specs=VM,
        scratch_shapes=[pltpu.SemaphoreType.DMA((n - 1,)), pltpu.SemaphoreType.DMA((n - 1,))],
        compiler_params=pltpu.CompilerParams(collective_id=collective_id, has_side_effects=True),
    )(x)


def on_device(
    genotypes, effects, gaussian_draw, prior_prec, accept,
    herd_effect, phenotype, record_animal, record_bin, live_records,
):
    step_size = 0.005
    rd, own = phenotype.shape[0], genotypes.shape[0]
    first_bin = (lax.axis_index("rec") * herd_effect.shape[0]).astype(jnp.int32).reshape(1)
    first_animal = (lax.axis_index("ani") * own).astype(jnp.int32).reshape(1)
    rows = pl.pallas_call(
        row_kernel,
        out_shape=shape(2, rd // W, W),
        in_specs=[SM, SM, VM, VM, VM, VM],
        out_specs=VM,
    )(
        first_bin, live_records, phenotype.reshape(-1, W), record_animal.reshape(-1, W),
        record_bin.reshape(-1, W), herd_effect.reshape(16, 128),
    )
    records = spread(rows, 1)
    breeding = jnp.dot(genotypes, effects.astype(BF16), preferred_element_type=F32)
    s, n = pl.pallas_call(
        scatter_kernel,
        out_shape=(shape(own // 128, 128), shape(own // 128, 128)),
        in_specs=[SM, VM],
        out_specs=(VM, VM),
        scratch_shapes=[pltpu.VMEM((384, 256), F32)],
    )(first_animal, records)
    dma = pltpu.SemaphoreType.DMA
    part = (NX, NZ, 8, 128)
    resid_sum = pl.pallas_call(
        exchange_kernel,
        out_shape=shape(*part),
        in_specs=[VM, VM, VM],
        out_specs=VM,
        scratch_shapes=[
            pltpu.VMEM((NX - 1, 3, NZ, 8, 128), F32),
            pltpu.VMEM((NZ, 3, 8, 128), F32),
            pltpu.VMEM((NZ - 1, 3, 8, 128), F32),
            dma((NX - 1, 3)), dma((NX - 1, 3)),
            dma((NZ - 1,)), dma((NZ - 1,)),
            dma((NZ - 1,)), dma((NZ - 1,)),
            dma((NX - 1,)), dma((NX - 1,)),
        ],
        compiler_params=pltpu.CompilerParams(collective_id=0, has_side_effects=True),
    )(breeding.reshape(part), s.reshape(part), n.reshape(part)).reshape(own)
    grad_part = jnp.dot(resid_sum.astype(BF16), genotypes, preferred_element_type=F32)
    g = spread(jnp.broadcast_to(grad_part, (8, 128)), 2)[:, 0]
    gradient = (g[0] + g[1]) + (g[2] + g[3]) - prior_prec * effects
    proposal = effects + step_size * gradient + math.sqrt(2.0 * step_size) * gaussian_draw
    accepted = jnp.repeat(accept, BLOCK) == 1
    return (jnp.where(accepted, proposal, effects), resid_sum)


def solution(mesh):
    return jax.shard_map(
        on_device,
        mesh=mesh,
        in_specs=(
            P("ani", "rec"),
            P(("chain", "rec")),
            P(("chain", "rec")),
            P("rec"),
            P(("chain", "rec")),
            P(("chain", "rec")),
            P(("rec", "ani")),
            P(("rec", "ani")),
            P(("rec", "ani")),
            P(("rec", "ani")),
        ),
        out_specs=(P(("chain", "rec")), P(("chain", "ani"))),
        check_vma=False,
    )
```
